32 devices in a mesh: head: 4 (over z), outer: 2 (over core), inner: 4 (over y, x).
Axes of the slice: x: 2, y: 2, z: 4, core: 2. Of those that a mesh axis runs over, the one named last changes fastest.
Arguments:
- query_in: bfloat16 [8, 384, 1024], P(('outer', 'inner'), 'head'), may hold values from -48 to 48
- key_in: bfloat16 [8, 384, 512], P(('outer', 'inner'), 'head'), may hold values from -6 to 6
- value_in: bfloat16 [8, 384, 512], P(('outer', 'inner'), 'head'), may hold values from -6 to 6
- grad_out: bfloat16 [8, 384, 1024], P(('outer', 'inner'), 'head'), may hold values from -48 to 48
Outputs:
- grad_query: bfloat16 [8, 384, 1024], P(('outer', 'inner'), 'head')
- grad_key: bfloat16 [8, 384, 512], P(('outer', 'inner'), 'head')
- grad_value: bfloat16 [8, 384, 512], P(('outer', 'inner'), 'head')
The draws below stay inside these ranges and needn't reach their ends.
All inputs are finite; a program needn't handle non-finite values.
Results may differ from the reference program's by a relative error of at most 0.0058.
Values may be sent and summed in bfloat16 or wider, within the bound.
A program may use at most 128 MiB of HBM per device.

```python
import jax
import jax.numpy as jnp
from jax import lax

HD = 128
GROUP = 2
WINDOW = 4096
T_DEV = 384
KV_HEADS = 4
Q_HEADS = 8
CTXB = 8


def draw_query_in(key, part):
    base_key = jax.random.fold_in(key, 11)
    mask_key = jax.random.fold_in(key, 12)
    size_key = jax.random.fold_in(key, 13)
    shape = (CTXB, T_DEV, Q_HEADS, HD)
    row_shape = (CTXB, T_DEV, Q_HEADS, 1)
    base = jax.random.normal(base_key, shape, jnp.float32) * 1.6
    spiked = jax.random.bernoulli(mask_key, 0.03, row_shape)
    factor = jnp.exp(jax.random.uniform(size_key, row_shape, jnp.float32, 1.7917595, 2.6390573))
    values = base * jnp.where(spiked, factor, 1.0)
    values = jnp.clip(values, -48.0, 48.0)
    return values.reshape(CTXB, T_DEV, Q_HEADS * HD).astype(jnp.bfloat16)


def shard_levels(rng, dims, cuts, least, top_value):
    gain = 1.0
    for position, shards_of in cuts:
        steps = jax.random.uniform(jax.random.fold_in(jax.random.fold_in(rng, 6), position), (shards_of,), jnp.float32, least / len(cuts), top_value / len(cuts))
        gain = gain * jnp.repeat(jnp.exp(steps), dims[position] // shards_of).reshape((-1,) + (1,) * (len(dims) - 1 - position))
    return gain


def bell_draw(stream_key, extent, scale, limit, split=(), kind=jnp.bfloat16):
    gain = shard_levels(stream_key, extent, split, -0.22, 0.18) if split else 1.0
    values = jax.random.normal(stream_key, extent, jnp.float32) * scale * gain
    return jnp.minimum(jnp.maximum(values, -limit), limit).astype(kind)


def setup_inputs(seed: int = 0) -> dict:
    key_list = jax.random.split(jax.random.key(seed), 5)
    return {
        "query_in": draw_query_in(jax.random.fold_in(key_list[4], 71), 0),
        "key_in": bell_draw(key_list[1], (CTXB, T_DEV, KV_HEADS * HD), 1.0, 6.0, ((0, 8), (1, 4))),
        "value_in": bell_draw(key_list[2], (CTXB, T_DEV, KV_HEADS * HD), 1.0, 6.0, ((0, 8), (1, 4))),
        "grad_out": bell_draw(key_list[3], (CTXB, T_DEV, Q_HEADS * HD), 8.0, 48.0, ((0, 8), (1, 4))),
    }


SOFT_CAP = 50.0
QUERY_SCALE = 1.0 / 12.0


def reference(query_in, key_in, value_in, grad_out):
    tok_rows = T_DEV
    lookback = (WINDOW + T_DEV - 2) // T_DEV
    key_span = (lookback + 1) * tok_rows
    all_rows = CTXB * tok_rows
    pad_rows = lookback * tok_rows
    query_all = query_in.reshape(all_rows, KV_HEADS, GROUP, HD)
    grad_all = grad_out.reshape(all_rows, KV_HEADS, GROUP, HD)
    key_all = jnp.concatenate([jnp.zeros((pad_rows, KV_HEADS, HD), key_in.dtype), key_in.reshape(all_rows, KV_HEADS, HD)], axis=0)
    value_all = jnp.concatenate([jnp.zeros((pad_rows, KV_HEADS, HD), value_in.dtype), value_in.reshape(all_rows, KV_HEADS, HD)], axis=0)

    def per_block(grad_sum, block_index):
        row_start = (block_index * tok_rows).astype(jnp.int32)
        query_blk = lax.dynamic_slice_in_dim(query_all, row_start, tok_rows, 0).astype(jnp.float32)
        grad_blk = lax.dynamic_slice_in_dim(grad_all, row_start, tok_rows, 0).astype(jnp.float32)
        key_blk = lax.dynamic_slice_in_dim(key_all, row_start, key_span, 0).astype(jnp.float32)
        value_blk = lax.dynamic_slice_in_dim(value_all, row_start, key_span, 0).astype(jnp.float32)
        scores = jnp.einsum("tagd,kad->agtk", query_blk, key_blk)
        capped = jnp.tanh(scores * (QUERY_SCALE / SOFT_CAP))
        grad_prob = jnp.einsum("tagd,kad->agtk", grad_blk, value_blk)
        grad_prob = lax.optimization_barrier(grad_prob.astype(jnp.bfloat16)).astype(jnp.float32)
        query_pos = row_start + lax.broadcasted_iota(jnp.int32, (tok_rows, key_span), 0)
        key_pos = row_start - pad_rows + lax.broadcasted_iota(jnp.int32, (tok_rows, key_span), 1)
        allowed = (key_pos <= query_pos) & (key_pos > query_pos - WINDOW) & (key_pos >= 0)
        weights = jnp.where(allowed, jnp.exp(SOFT_CAP * capped), 0.0)
        totals = jnp.sum(weights, axis=3)
        row_delta = jnp.sum(weights * grad_prob, axis=3) / totals
        attn_prob = weights / totals[..., None]
        prob_round = lax.optimization_barrier(attn_prob.astype(jnp.bfloat16)).astype(jnp.float32)
        grad_value = jnp.einsum("agtk,tagd->kad", prob_round, grad_blk)
        scaled = attn_prob * (grad_prob - row_delta[..., None]) * (QUERY_SCALE * (1.0 - capped * capped))
        scaled = lax.optimization_barrier(scaled.astype(jnp.bfloat16)).astype(jnp.float32)
        grad_query = jnp.einsum("agtk,kad->tagd", scaled, key_blk)
        grad_key = jnp.einsum("agtk,tagd->kad", scaled, query_blk)
        kv_grads = jnp.stack([grad_key, grad_value], axis=2)
        current = lax.dynamic_slice_in_dim(grad_sum, row_start, key_span, 0)
        grad_sum = lax.dynamic_update_slice_in_dim(grad_sum, current + kv_grads, row_start, 0)
        return grad_sum, grad_query

    grad_init = jnp.zeros((pad_rows + all_rows, KV_HEADS, 2, HD), jnp.float32)
    grad_sum, query_grads = lax.scan(per_block, grad_init, jnp.arange(CTXB, dtype=jnp.int32))
    grad_query = query_grads.reshape(CTXB, tok_rows, Q_HEADS * HD).astype(jnp.bfloat16)
    grad_key = grad_sum[pad_rows:, :, 0].reshape(CTXB, tok_rows, KV_HEADS * HD).astype(jnp.bfloat16)
    grad_value = grad_sum[pad_rows:, :, 1].reshape(CTXB, tok_rows, KV_HEADS * HD).astype(jnp.bfloat16)
    return (grad_query, grad_key, grad_value)
```

```python
import functools

import jax
import jax.numpy as jnp
from jax import lax
from jax.experimental import pallas as pl
from jax.experimental.pallas import tpu as pltpu
from jax.sharding import PartitionSpec as P

HD = 128
GROUP = 2
WINDOW = 4096
SOFT_CAP = 50.0
QUERY_SCALE = 1.0 / 12.0
LOG2E = 1.4426950408889634
MESH = pl.DeviceIdType.MESH
KT = 128
ORDER = (2, 3)


def dot(a, b, ca, cb):
    return lax.dot_general(a, b, (((ca,), (cb,)), ((), ())), preferred_element_type=jnp.float32)


def kernel(
    heads, outer_n, inner_n, back, lap,
    q_in, k_in, v_in, g_in,
    q_out, k_out, v_out,
    qs, gs, qst, gst, kv, e_all, w_all, d_all, tot, wgt, dqt, dq, dkv, part_sum, dsend, drecv, lent, own,
    a_send, a_recv, a_loc, b_send, b_recv, f_send, d_ssem, d_rsem, r_rsem, e_send, e_recv, e_loc, gate,
):
    rows = q_in.shape[0]
    tok = rows * heads
    ctx = outer_n * inner_n
    h = lax.axis_index("head")
    pos = lax.axis_index("outer") * inner_n + lax.axis_index("inner")
    reach = jnp.minimum(pos, back)
    beyond = jnp.minimum(ctx - 1 - pos, back)

    def is_late(t):
        return lax.rem(lax.div(t, inner_n), 2) == 1

    late = is_late(pos)
    twin = lax.rem(jnp.where(late, pos - inner_n, pos + inner_n) + ctx, ctx)

    def at(t):
        return {"outer": lax.div(t, inner_n), "inner": lax.rem(t, inner_n)}

    def head_at(d):
        return lax.rem(h + d, heads)

    def part(who):
        return pl.ds(pl.multiple_of(who * rows, rows), rows)

    def lanes(who, width):
        return pl.ds(pl.multiple_of(who * width, width), width)

    barrier = pltpu.get_barrier_semaphore()
    for d in range(1, heads):
        pl.semaphore_signal(barrier, inc=1, device_id={"head": head_at(d)}, device_id_type=MESH)
    for s in range(1, back + 1):
        @pl.when(pos + s < ctx)
        def _():
            pl.semaphore_signal(barrier, inc=1, device_id=at(pos + s), device_id_type=MESH)

        @pl.when(pos - s >= 0)
        def _():
            pl.semaphore_signal(barrier, inc=1, device_id=at(pos - s), device_id_type=MESH)
    pl.semaphore_wait(barrier, heads - 1 + reach + beyond)

    srcs = ((k_in, HD), (v_in, HD), (q_in, GROUP * HD), (g_in, GROUP * HD))

    def dst_a(kind, who):
        if kind < 2:
            return kv.at[0, kind, part(who)]
        return (qs if kind == 2 else gs).at[part(who)]

    def copy_a(kind, d):
        ref, width = srcs[kind]
        return pltpu.make_async_remote_copy(
            src_ref=ref.at[:, lanes(head_at(d), width)],
            dst_ref=dst_a(kind, h),
            send_sem=a_send.at[kind, d], recv_sem=a_recv.at[kind, d],
            device_id={"head": head_at(d)}, device_id_type=MESH,
        )

    def arrival_a(kind, d):
        ref, width = srcs[kind]
        return pltpu.make_async_remote_copy(
            src_ref=ref.at[:, lanes(h, width)],
            dst_ref=dst_a(kind, head_at(heads - d)),
            send_sem=a_send.at[kind, d], recv_sem=a_recv.at[kind, d],
            device_id={"head": head_at(d)}, device_id_type=MESH,
        )

    def local_a(kind):
        ref, width = srcs[kind]
        return pltpu.make_async_copy(ref.at[:, lanes(h, width)], dst_a(kind, h), a_loc.at[kind])

    def start_a(kind):
        for d in range(1, heads):
            copy_a(kind, d).start()

    def landed_a(kind):
        local_a(kind).wait()
        for d in range(1, heads):
            arrival_a(kind, d).wait_recv()

    for kind in (0, 1):
        start_a(kind)
    for kind in ORDER:
        if lap >= 0:
            @pl.when(late)
            def _():
                start_a(kind)
        else:
            start_a(kind)
    for kind in range(4):
        local_a(kind).start()

    def straight(s):
        if lap < 1:
            return pos + s < ctx
        return (pos + s < ctx) & ((s > lap) | is_late(pos + s))

    def copy_b(kind, s):
        return pltpu.make_async_remote_copy(
            src_ref=kv.at[0, kind], dst_ref=kv.at[s, kind],
            send_sem=b_send.at[kind, s], recv_sem=b_recv.at[kind, s],
            device_id=at(lax.rem(pos + s, ctx)), device_id_type=MESH,
        )

    def copy_f(kind, s):
        return pltpu.make_async_remote_copy(
            src_ref=kv.at[s, kind], dst_ref=kv.at[s - inner_n, kind],
            send_sem=f_send.at[kind, s - inner_n], recv_sem=b_recv.at[kind, s - inner_n],
            device_id=at(twin), device_id_type=MESH,
        )

    def landed_b(kind, s):
        copy_b(kind, s).wait_recv()
        if lap >= 1:
            @pl.when(late & (s > inner_n))
            def _():
                copy_f(kind, s).start()

    for kind in (0, 1):
        landed_a(kind)
        for s in range(1, back + 1):
            @pl.when(straight(s))
            def _():
                copy_b(kind, s).start()

    if lap >= 0:
        @pl.when(jnp.logical_not(late))
        def _():
            pl.semaphore_wait(gate, 1)
            for kind in ORDER:
                start_a(kind)

    tot[...] = jnp.zeros_like(tot)
    wgt[...] = jnp.zeros_like(wgt)
    dqt[...] = jnp.zeros_like(dqt)

    free = (WINDOW - tok) // tok

    def first(s, masked):
        for t in range(tok // KT):
            at_t = slice(t * KT, (t + 1) * KT)
            keys = kv[s, 0, at_t]
            for j in range(GROUP):
                col = slice(j * tok, (j + 1) * tok)
                capped = jnp.tanh(dot(keys, qst[col], 1, 1) * (QUERY_SCALE / SOFT_CAP))
                e = jnp.exp2((SOFT_CAP * LOG2E) * capped)
                if masked:
                    apart = (
                        s * tok - t * KT
                        + lax.broadcasted_iota(jnp.int32, e.shape, 1)
                        - lax.broadcasted_iota(jnp.int32, e.shape, 0)
                    )
                    e = jnp.where((apart >= 0) & (apart < WINDOW), e, 0.0)
                w_all[s, at_t, col] = e * (QUERY_SCALE - QUERY_SCALE * (capped * capped))
                e_all[s, at_t, col] = e
                tot[:, col] += jnp.sum(e.reshape(KT // 8, 8, tok), axis=0)

    def copy_d(s, which):
        return pltpu.make_async_remote_copy(
            src_ref=dsend.at[s - 1, which], dst_ref=drecv.at[s - 1, which],
            send_sem=d_ssem.at[s - 1, which], recv_sem=d_rsem.at[s - 1, which],
            device_id=at(lax.rem(pos - s + ctx, ctx)), device_id_type=MESH,
        )

    def copy_r(s, which):
        return pltpu.make_async_remote_copy(
            src_ref=dsend.at[s - 1, which], dst_ref=lent.at[s - inner_n - 1, which],
            send_sem=d_ssem.at[s - 1, which], recv_sem=r_rsem.at[s - inner_n - 1, which],
            device_id=at(twin), device_id_type=MESH,
        )

    def arrival_r(s, which):
        return pltpu.make_async_remote_copy(
            src_ref=dsend.at[s - 1, which], dst_ref=lent.at[s - 1, which],
            send_sem=d_ssem.at[s - 1, which], recv_sem=r_rsem.at[s - 1, which],
            device_id=at(twin), device_id_type=MESH,
        )

    def give(s, which, value):
        if lap < 1:
            dsend[s - 1, which] = value.astype(jnp.bfloat16)
            copy_d(s, which).start()
            return
        part_sum[...] = value

        @pl.when(jnp.logical_not(late) & (s <= lap))
        def _():
            arrival_r(s, which).wait_recv()
            part_sum[...] += lent[s - 1, which].astype(jnp.float32)

        dsend[s - 1, which] = part_sum[...].astype(jnp.bfloat16)
        lend = late & (s > inner_n)

        @pl.when(lend)
        def _():
            copy_r(s, which).start()

        @pl.when(jnp.logical_not(lend))
        def _():
            copy_d(s, which).start()

    def first_dp(s):
        dvs = []
        for t in range(tok // KT):
            at_t = slice(t * KT, (t + 1) * KT)
            vals = kv[s, 1, at_t]
            probs = []
            for j in range(GROUP):
                col = slice(j * tok, (j + 1) * tok)
                dp = dot(vals, gst[col], 1, 1).astype(jnp.bfloat16)
                d_all[s, at_t, col] = dp
                e = e_all[s, at_t, col]
                weighted = e * dp.astype(jnp.float32)
                wgt[:, col] += jnp.sum(weighted.reshape(KT // 8, 8, tok), axis=0)
                probs.append((e * tot[0:1, col]).astype(jnp.bfloat16))
            dvs.append(dot(jnp.concatenate(probs, axis=1), gst[...], 1, 0))
        return jnp.concatenate(dvs, axis=0)

    def stack(whole, stacked):
        for j in range(GROUP):
            stacked[j * tok:(j + 1) * tok] = whole[:, j * HD:(j + 1) * HD]

    landed_a(2)
    if lap >= 0:
        @pl.when(late)
        def _():
            pl.semaphore_signal(gate, inc=1, device_id=at(twin), device_id_type=MESH)
    stack(qs, qst)
    first(0, True)

    def first_step(masked, s, carry):
        landed_b(0, s)
        first(s, masked)
        return carry

    edge = jnp.minimum(reach, free)
    lax.fori_loop(1, edge + 1, functools.partial(first_step, False), 0)
    if back > free:
        lax.fori_loop(edge + 1, reach + 1, functools.partial(first_step, True), 0)
    inv = 1.0 / jnp.sum(tot[...], axis=0, keepdims=True)
    tot[0:1] = inv
    landed_a(3)
    stack(gs, gst)

    def first_dp_step(s, carry):
        landed_b(1, s)
        give(s, 1, first_dp(s))
        return carry

    own[1] = first_dp(0)
    lax.fori_loop(1, reach + 1, first_dp_step, 0)

    delta = jnp.sum(wgt[...], axis=0, keepdims=True) * tot[0:1]
    wgt[0:1] = delta

    def second(s):
        dks = []
        for t in range(tok // KT):
            at_t = slice(t * KT, (t + 1) * KT)
            scs = []
            for j in range(GROUP):
                col = slice(j * tok, (j + 1) * tok)
                diff = d_all[s, at_t, col].astype(jnp.float32) - wgt[0:1, col]
                scs.append(((w_all[s, at_t, col] * tot[0:1, col]) * diff).astype(jnp.bfloat16))
            scaled = jnp.concatenate(scs, axis=1)
            dks.append(dot(scaled, qst[...], 1, 0))
            dqt[...] += dot(kv[s, 0, at_t], scaled, 0, 0)
        return jnp.concatenate(dks, axis=0)

    def second_step(i, carry):
        s = reach - i
        give(s, 0, second(s))
        return carry

    lax.fori_loop(0, reach, second_step, 0)
    own[0] = second(0)
    for j in range(GROUP):
        dq[:, j * HD:(j + 1) * HD] = dqt[:, j * tok:(j + 1) * tok].T.astype(jnp.bfloat16)

    outs = ((q_out, GROUP * HD), (k_out, HD), (v_out, HD))

    def src_e(kind, who):
        return dq.at[part(who)] if kind == 0 else dkv.at[kind - 1, part(who)]

    def copy_e(kind, d):
        ref, width = outs[kind]
        return pltpu.make_async_remote_copy(
            src_ref=src_e(kind, head_at(d)), dst_ref=ref.at[:, lanes(h, width)],
            send_sem=e_send.at[kind, d], recv_sem=e_recv.at[kind, d],
            device_id={"head": head_at(d)}, device_id_type=MESH,
        )

    def arrival_e(kind, d):
        ref, width = outs[kind]
        return pltpu.make_async_remote_copy(
            src_ref=src_e(kind, h), dst_ref=ref.at[:, lanes(head_at(heads - d), width)],
            send_sem=e_send.at[kind, d], recv_sem=e_recv.at[kind, d],
            device_id={"head": head_at(d)}, device_id_type=MESH,
        )

    def local_e(kind):
        ref, width = outs[kind]
        return pltpu.make_async_copy(src_e(kind, h), ref.at[:, lanes(h, width)], e_loc.at[kind])

    def start_e(kind):
        for d in range(1, heads):
            copy_e(kind, d).start()
        local_e(kind).start()

    start_e(0)

    def collect(which, s, carry):
        def take():
            copy_d(s, which).wait_recv()
            own[which] += drecv[s - 1, which].astype(jnp.float32)

        if lap < 1:
            take()
        else:
            pl.when(jnp.logical_not(is_late(pos + s) & (s > inner_n)))(take)
        return carry

    for which in (1, 0):
        lax.fori_loop(1, beyond + 1, functools.partial(collect, which), 0)
        dkv[which] = own[which].astype(jnp.bfloat16)
        start_e(which + 1)

    for kind in range(4):
        for d in range(1, heads):
            copy_a(kind, d).wait_send()

    def sent_b(s, carry):
        @pl.when(straight(s))
        def _():
            for kind in (0, 1):
                copy_b(kind, s).wait_send()
        return carry

    lax.fori_loop(1, beyond + 1, sent_b, 0)
    if lap >= 1:
        def sent_f(s, carry):
            for kind in (0, 1):
                copy_f(kind, s).wait_send()
            return carry

        @pl.when(late)
        def _():
            lax.fori_loop(inner_n + 1, reach + 1, sent_f, 0)

    def sent_d(s, carry):
        for which in (0, 1):
            copy_d(s, which).wait_send()
        return carry

    lax.fori_loop(1, reach + 1, sent_d, 0)
    for kind in range(3):
        local_e(kind).wait()
        for d in range(1, heads):
            copy_e(kind, d).wait_send()
            arrival_e(kind, d).wait_recv()


def hand_on(a, b, c, a_to, b_to, c_to, a_via, b_via, c_via, sems):
    ways = ((a, a_via, a_to), (b, b_via, b_to), (c, c_via, c_to))
    into = [pltpu.make_async_copy(x, v, sems.at[0, i]) for i, (x, v, _) in enumerate(ways)]
    out = [pltpu.make_async_copy(v, y, sems.at[1, i]) for i, (_, v, y) in enumerate(ways)]
    for copy in into:
        copy.start()
    for before, after in zip(into, out):
        before.wait()
        after.start()
    for copy in out:
        copy.wait()


def solution(mesh):
    heads, outer_n, inner_n = (mesh.shape[a] for a in ("head", "outer", "inner"))

    def body(query_in, key_in, value_in, grad_out):
        rows = query_in.shape[1]
        tok = rows * heads
        back = min((WINDOW + tok - 2) // tok, outer_n * inner_n - 1)
        lap = back - inner_n if outer_n % 2 == 0 else -1
        lent = max(lap, 1)
        wide = GROUP * tok
        bf16, f32 = jnp.bfloat16, jnp.float32
        sem = pltpu.SemaphoreType.DMA
        shapes = [(query_in.shape[1:]), (key_in.shape[1:]), (value_in.shape[1:])]
        res = pl.pallas_call(
            functools.partial(kernel, heads, outer_n, inner_n, back, lap),
            out_shape=[jax.ShapeDtypeStruct(s, bf16) for s in shapes],
            in_specs=[pl.BlockSpec(memory_space=pl.ANY)] * 4,
            out_specs=[pl.BlockSpec(memory_space=pl.ANY)] * 3,
            scratch_shapes=[
                pltpu.VMEM((tok, GROUP * HD), bf16),
                pltpu.VMEM((tok, GROUP * HD), bf16),
                pltpu.VMEM((wide, HD), bf16),
                pltpu.VMEM((wide, HD), bf16),
                pltpu.VMEM((back + 1, 2, tok, HD), bf16),
                pltpu.VMEM((back + 1, tok, wide), f32),
                pltpu.VMEM((back + 1, tok, wide), f32),
                pltpu.VMEM((back + 1, tok, wide), bf16),
                pltpu.VMEM((8, wide), f32),
                pltpu.VMEM((8, wide), f32),
                pltpu.VMEM((HD, wide), f32),
                pltpu.VMEM((tok, GROUP * HD), bf16),
                pltpu.VMEM((2, tok, HD), bf16),
                pltpu.VMEM((tok, HD), f32),
                pltpu.VMEM((back, 2, tok, HD), bf16),
                pltpu.VMEM((back, 2, tok, HD), bf16),
                pltpu.VMEM((lent, 2, tok, HD), bf16),
                pltpu.VMEM((2, tok, HD), f32),
                sem((4, heads)), sem((4, heads)), sem((4,)),
                sem((2, back + 1)), sem((2, back + 1)), sem((2, lent + 1)),
                sem((back, 2)), sem((back, 2)), sem((lent, 2)),
                sem((3, heads)), sem((3, heads)), sem((3,)),
                pltpu.SemaphoreType.REGULAR,
            ],
            compiler_params=pltpu.CompilerParams(
                collective_id=0, has_side_effects=True, vmem_limit_bytes=60 * 1024 * 1024
            ),
        )(query_in[0], key_in[0], value_in[0], grad_out[0])
        res = pl.pallas_call(
            hand_on,
            out_shape=[jax.ShapeDtypeStruct(s, bf16) for s in shapes],
            in_specs=[pl.BlockSpec(memory_space=pl.ANY)] * 3,
            out_specs=[pl.BlockSpec(memory_space=pl.ANY)] * 3,
            scratch_shapes=[pltpu.VMEM(s, bf16) for s in shapes] + [sem((2, 3))],
        )(*res)
        return tuple(r[None] for r in res)

    spec = P(("outer", "inner"), "head", None)
    return jax.shard_map(
        body, mesh=mesh, in_specs=(spec,) * 4, out_specs=(spec,) * 3, check_vma=False
    )
```

```python
import functools

import jax
import jax.numpy as jnp
from jax import lax
from jax.experimental import pallas as pl
from jax.experimental.pallas import tpu as pltpu
from jax.sharding import PartitionSpec as P

HD = 128
GROUP = 2
WINDOW = 4096
SOFT_CAP = 50.0
QUERY_SCALE = 1.0 / 12.0
LOG2E = 1.4426950408889634
MESH = pl.DeviceIdType.MESH
KT = 128
QT = 256


def dot(a, b, ca, cb):
    return lax.dot_general(a, b, (((ca,), (cb,)), ((), ())), preferred_element_type=jnp.float32)


def kernel(
    heads, outer_n, inner_n, back, lap,
    q_in, k_in, v_in, g_in,
    q_out, k_out, v_out,
    qs, gs, qst, gst, kv, e_all, w_all, d_all, tot, wgt, dqt, dq, dkv, part_sum, dsend, drecv, lent, own,
    a_send, a_recv, a_loc, b_send, b_recv, f_send, d_ssem, d_rsem, r_rsem, e_send, e_recv, e_loc,
):
    rows = q_in.shape[0]
    tok = rows * heads
    ctx = outer_n * inner_n
    h = lax.axis_index("head")
    pos = lax.axis_index("outer") * inner_n + lax.axis_index("inner")
    reach = jnp.minimum(pos, back)
    beyond = jnp.minimum(ctx - 1 - pos, back)

    def is_late(t):
        return lax.rem(lax.div(t, inner_n), 2) == 1

    late = is_late(pos)
    twin = lax.rem(jnp.where(late, pos - inner_n, pos + inner_n) + ctx, ctx)

    def at(t):
        return {"outer": lax.div(t, inner_n), "inner": lax.rem(t, inner_n)}

    def head_at(d):
        return lax.rem(h + d, heads)

    def part(who):
        return pl.ds(pl.multiple_of(who * rows, rows), rows)

    def lanes(who, width):
        return pl.ds(pl.multiple_of(who * width, width), width)

    barrier = pltpu.get_barrier_semaphore()
    for d in range(1, heads):
        pl.semaphore_signal(barrier, inc=1, device_id={"head": head_at(d)}, device_id_type=MESH)
    for s in range(1, back + 1):
        @pl.when(pos + s < ctx)
        def _():
            pl.semaphore_signal(barrier, inc=1, device_id=at(pos + s), device_id_type=MESH)

        @pl.when(pos - s >= 0)
        def _():
            pl.semaphore_signal(barrier, inc=1, device_id=at(pos - s), device_id_type=MESH)
    pl.semaphore_wait(barrier, heads - 1 + reach + beyond)

    srcs = ((k_in, HD), (v_in, HD), (q_in, GROUP * HD), (g_in, GROUP * HD))

    def dst_a(kind, who):
        if kind < 2:
            return kv.at[kind, 0, part(who)]
        return (qs if kind == 2 else gs).at[part(who)]

    def copy_a(kind, d):
        ref, width = srcs[kind]
        return pltpu.make_async_remote_copy(
            src_ref=ref.at[:, lanes(head_at(d), width)],
            dst_ref=dst_a(kind, h),
            send_sem=a_send.at[kind, d], recv_sem=a_recv.at[kind, d],
            device_id={"head": head_at(d)}, device_id_type=MESH,
        )

    def arrival_a(kind, d):
        ref, width = srcs[kind]
        return pltpu.make_async_remote_copy(
            src_ref=ref.at[:, lanes(h, width)],
            dst_ref=dst_a(kind, head_at(heads - d)),
            send_sem=a_send.at[kind, d], recv_sem=a_recv.at[kind, d],
            device_id={"head": head_at(d)}, device_id_type=MESH,
        )

    def local_a(kind):
        ref, width = srcs[kind]
        return pltpu.make_async_copy(ref.at[:, lanes(h, width)], dst_a(kind, h), a_loc.at[kind])

    def start_a(kind):
        for d in range(1, heads):
            copy_a(kind, d).start()

    def landed_a(kind):
        local_a(kind).wait()
        for d in range(1, heads):
            arrival_a(kind, d).wait_recv()

    start_a(0)

    @pl.when(late)
    def _():
        for kind in (1, 2, 3):
            start_a(kind)

    @pl.when(jnp.logical_not(late))
    def _():
        start_a(1)

    for kind in range(4):
        local_a(kind).start()

    def straight(s):
        if lap < 1:
            return pos + s < ctx
        return (pos + s < ctx) & ((s > lap) | is_late(pos + s))

    def copy_b(kind, s):
        return pltpu.make_async_remote_copy(
            src_ref=kv.at[kind, 0], dst_ref=kv.at[kind, s],
            send_sem=b_send.at[kind, s], recv_sem=b_recv.at[kind, s],
            device_id=at(lax.rem(pos + s, ctx)), device_id_type=MESH,
        )

    def copy_f(kind, s):
        return pltpu.make_async_remote_copy(
            src_ref=kv.at[kind, s], dst_ref=kv.at[kind, s - inner_n],
            send_sem=f_send.at[kind, s - inner_n], recv_sem=b_recv.at[kind, s - inner_n],
            device_id=at(twin), device_id_type=MESH,
        )

    def landed_b(kind, s):
        copy_b(kind, s).wait_recv()
        if lap >= 1:
            @pl.when(late & (s > inner_n))
            def _():
                copy_f(kind, s).start()

    tot[...] = jnp.zeros_like(tot)
    wgt[...] = jnp.zeros_like(wgt)
    dqt[...] = jnp.zeros_like(dqt)

    free = (WINDOW - tok) // tok

    def blocks(s, n):
        return pl.ds(pl.multiple_of(s * tok, tok), n * tok)

    def first(s, n, masked):
        at_s = blocks(s, n)
        keys = kv[0, pl.ds(s, n)].reshape(n * tok, HD)
        for j in range(GROUP * tok // QT):
            col = slice(j * QT, (j + 1) * QT)
            capped = jnp.tanh(dot(keys, qst[col], 1, 1) * (QUERY_SCALE / SOFT_CAP))
            e = jnp.exp2((SOFT_CAP * LOG2E) * capped)
            if masked:
                query = j * QT + lax.broadcasted_iota(jnp.int32, e.shape, 1)
                apart = (
                    s * tok + jnp.where(query >= tok, query - tok, query)
                    - lax.broadcasted_iota(jnp.int32, e.shape, 0)
                )
                e = jnp.where((apart >= 0) & (apart < WINDOW), e, 0.0)
            w_all[at_s, col] = e * (QUERY_SCALE - QUERY_SCALE * (capped * capped))
            e_all[at_s, col] = e
            tot[:, col] += jnp.sum(e.reshape(n * tok // 8, 8, QT), axis=0)

    def seen(t):
        return [slice(j * tok + t * KT, (j + 1) * tok) for j in range(GROUP)]

    def first_own():
        for t in range(tok // KT):
            at_t = slice(t * KT, (t + 1) * KT)
            keys = kv[0, 0, at_t]
            for col in seen(t):
                capped = jnp.tanh(dot(keys, qst[col], 1, 1) * (QUERY_SCALE / SOFT_CAP))
                e = jnp.exp2((SOFT_CAP * LOG2E) * capped)
                apart = (
                    lax.broadcasted_iota(jnp.int32, e.shape, 1)
                    - lax.broadcasted_iota(jnp.int32, e.shape, 0)
                )
                e = jnp.where(apart >= 0, e, 0.0)
                w_all[at_t, col] = e * (QUERY_SCALE - QUERY_SCALE * (capped * capped))
                e_all[at_t, col] = e
                tot[:, col] += jnp.sum(e.reshape(KT // 8, 8, e.shape[1]), axis=0)

    def copy_d(s, which):
        return pltpu.make_async_remote_copy(
            src_ref=dsend.at[s - 1, which], dst_ref=drecv.at[s - 1, which],
            send_sem=d_ssem.at[s - 1, which], recv_sem=d_rsem.at[s - 1, which],
            device_id=at(lax.rem(pos - s + ctx, ctx)), device_id_type=MESH,
        )

    def copy_r(s, which):
        return pltpu.make_async_remote_copy(
            src_ref=dsend.at[s - 1, which], dst_ref=lent.at[s - inner_n - 1, which],
            send_sem=d_ssem.at[s - 1, which], recv_sem=r_rsem.at[s - inner_n - 1, which],
            device_id=at(twin), device_id_type=MESH,
        )

    def arrival_r(s, which):
        return pltpu.make_async_remote_copy(
            src_ref=dsend.at[s - 1, which], dst_ref=lent.at[s - 1, which],
            send_sem=d_ssem.at[s - 1, which], recv_sem=r_rsem.at[s - 1, which],
            device_id=at(twin), device_id_type=MESH,
        )

    def give(s, n, which, value):
        part_sum[0:n * tok] = value
        for m in range(n):
            give_one(s + m, which, slice(m * tok, (m + 1) * tok))

    def give_one(s, which, rows_s):
        if lap < 1:
            dsend[s - 1, which] = part_sum[rows_s].astype(jnp.bfloat16)
            copy_d(s, which).start()
            return

        @pl.when(jnp.logical_not(late) & (s <= lap))
        def _():
            arrival_r(s, which).wait_recv()
            part_sum[rows_s] += lent[s - 1, which].astype(jnp.float32)

        dsend[s - 1, which] = part_sum[rows_s].astype(jnp.bfloat16)
        lend = late & (s > inner_n)

        @pl.when(lend)
        def _():
            copy_r(s, which).start()

        @pl.when(jnp.logical_not(lend))
        def _():
            copy_d(s, which).start()

    def first_dv(s, n):
        at_s = blocks(s, n)
        probs = [
            (e_all[at_s, j * QT:(j + 1) * QT] * tot[0:1, j * QT:(j + 1) * QT]).astype(jnp.bfloat16)
            for j in range(GROUP * tok // QT)
        ]
        give(s, n, 1, dot(jnp.concatenate(probs, axis=1), gst[...], 1, 0))

    def first_dv_own():
        for t in range(tok // KT):
            at_t = slice(t * KT, (t + 1) * KT)
            probs = [(e_all[at_t, col] * tot[0:1, col]).astype(jnp.bfloat16) for col in seen(t)]
            grads = jnp.concatenate([gst[col] for col in seen(t)], axis=0)
            own[1, at_t] = dot(jnp.concatenate(probs, axis=1), grads, 1, 0)

    def first_dp(s, n):
        for m in range(n):
            if lap >= 1:
                @pl.when(jnp.logical_not(late & (s + m > inner_n)))
                def _():
                    landed_b(1, s + m)
            else:
                landed_b(1, s + m)
        at_s = blocks(s, n)
        vals = kv[1, pl.ds(s, n)].reshape(n * tok, HD)
        for j in range(GROUP * tok // QT):
            col = slice(j * QT, (j + 1) * QT)
            dp = dot(vals, gst[col], 1, 1).astype(jnp.bfloat16)
            d_all[at_s, col] = dp
            weighted = e_all[at_s, col] * dp.astype(jnp.float32)
            wgt[:, col] += jnp.sum(weighted.reshape(n * tok // 8, 8, QT), axis=0)

    def first_dp_own():
        for t in range(tok // KT):
            at_t = slice(t * KT, (t + 1) * KT)
            vals = kv[1, 0, at_t]
            for col in seen(t):
                dp = dot(vals, gst[col], 1, 1).astype(jnp.bfloat16)
                d_all[at_t, col] = dp
                weighted = e_all[at_t, col] * dp.astype(jnp.float32)
                wgt[:, col] += jnp.sum(weighted.reshape(KT // 8, 8, weighted.shape[1]), axis=0)

    def stack(whole, stacked):
        for j in range(GROUP):
            stacked[j * tok:(j + 1) * tok] = whole[:, j * HD:(j + 1) * HD]

    def spread(kind):
        landed_a(kind)
        for s in range(1, back + 1):
            @pl.when(straight(s))
            def _():
                copy_b(kind, s).start()

    def begin():
        landed_a(2)
        stack(qs, qst)
        first_own()

    spread(0)

    pl.when(jnp.logical_not(late))(lambda: start_a(2))
    spread(1)
    pl.when(jnp.logical_not(late))(lambda: start_a(3))
    begin()

    def first_step(n, masked, base, i, carry):
        s = base + n * i
        for m in range(n):
            landed_b(0, s + m)
        first(s, n, masked)
        return carry

    edge = jnp.minimum(reach, free)
    lax.fori_loop(0, lax.div(edge, 2), functools.partial(first_step, 2, False, 1), 0)
    lax.fori_loop(edge, edge + lax.rem(edge, 2), functools.partial(first_step, 1, False, 0), 0)
    if back > free:
        lax.fori_loop(edge + 1, reach + 1, functools.partial(first_step, 1, True, 0), 0)
    inv = 1.0 / jnp.sum(tot[...], axis=0, keepdims=True)
    tot[0:1] = inv
    if lap >= 1:
        def pass_on(s, carry):
            landed_b(1, s)
            return carry

        @pl.when(late)
        def _():
            lax.fori_loop(inner_n + 1, reach + 1, pass_on, 0)
    landed_a(3)
    stack(gs, gst)

    def in_pairs(step, begin, end):
        def two(i, carry):
            step(reach - 2 * i - 1, 2)
            return carry

        lax.fori_loop(begin, end, two, 0)

    pairs = lax.div(reach, 2)

    def odd_one(step):
        @pl.when(lax.rem(reach, 2) == 1)
        def _():
            step(1, 1)

    in_pairs(first_dv, 0, pairs)
    odd_one(first_dv)
    first_dv_own()
    in_pairs(first_dp, 0, pairs)
    odd_one(first_dp)
    first_dp_own()

    delta = jnp.sum(wgt[...], axis=0, keepdims=True) * tot[0:1]
    wgt[0:1] = delta

    def second(s, n):
        at_s = blocks(s, n)
        keys = kv[0, pl.ds(s, n)].reshape(n * tok, HD)
        scs = []
        for j in range(GROUP * tok // QT):
            col = slice(j * QT, (j + 1) * QT)
            diff = d_all[at_s, col].astype(jnp.float32) - wgt[0:1, col]
            scaled = ((w_all[at_s, col] * tot[0:1, col]) * diff).astype(jnp.bfloat16)
            dqt[:, col] += dot(keys, scaled, 0, 0)
            scs.append(scaled)
        return dot(jnp.concatenate(scs, axis=1), qst[...], 1, 0)

    def second_own():
        for t in range(tok // KT):
            at_t = slice(t * KT, (t + 1) * KT)
            scs = []
            for col in seen(t):
                diff = d_all[at_t, col].astype(jnp.float32) - wgt[0:1, col]
                scaled = ((w_all[at_t, col] * tot[0:1, col]) * diff).astype(jnp.bfloat16)
                dqt[:, col] += dot(kv[0, 0, at_t], scaled, 0, 0)
                scs.append(scaled)
            queries = jnp.concatenate([qst[col] for col in seen(t)], axis=0)
            own[0, at_t] = dot(jnp.concatenate(scs, axis=1), queries, 1, 0)

    def second_at(s, n):
        give(s, n, 0, second(s, n))

    outs = ((q_out, GROUP * HD), (k_out, HD), (v_out, HD))

    def src_e(kind, who):
        return dq.at[part(who)] if kind == 0 else dkv.at[kind - 1, part(who)]

    def copy_e(kind, d):
        ref, width = outs[kind]
        return pltpu.make_async_remote_copy(
            src_ref=src_e(kind, head_at(d)), dst_ref=ref.at[:, lanes(h, width)],
            send_sem=e_send.at[kind, d], recv_sem=e_recv.at[kind, d],
            device_id={"head": head_at(d)}, device_id_type=MESH,
        )

    def arrival_e(kind, d):
        ref, width = outs[kind]
        return pltpu.make_async_remote_copy(
            src_ref=src_e(kind, h), dst_ref=ref.at[:, lanes(head_at(heads - d), width)],
            send_sem=e_send.at[kind, d], recv_sem=e_recv.at[kind, d],
            device_id={"head": head_at(d)}, device_id_type=MESH,
        )

    def local_e(kind):
        ref, width = outs[kind]
        return pltpu.make_async_copy(src_e(kind, h), ref.at[:, lanes(h, width)], e_loc.at[kind])

    def start_e(kind):
        for d in range(1, heads):
            copy_e(kind, d).start()
        local_e(kind).start()

    def collect(which, s, carry):
        def take():
            copy_d(s, which).wait_recv()
            own[which] += drecv[s - 1, which].astype(jnp.float32)

        if lap < 1:
            take()
        else:
            pl.when(jnp.logical_not(is_late(pos + s) & (s > inner_n)))(take)
        return carry

    def hand_back(which):
        lax.fori_loop(1, beyond + 1, functools.partial(collect, which), 0)
        dkv[which] = own[which].astype(jnp.bfloat16)
        start_e(which + 1)

    last = lax.rem(pos, inner_n) == inner_n - 1
    pl.when(last)(lambda: hand_back(1))
    in_pairs(second_at, 0, pairs)
    odd_one(second_at)
    second_own()
    for j in range(GROUP):
        dq[:, j * HD:(j + 1) * HD] = dqt[:, j * tok:(j + 1) * tok].T.astype(jnp.bfloat16)
    start_e(0)
    pl.when(jnp.logical_not(last))(lambda: hand_back(1))
    hand_back(0)

    for kind in range(4):
        for d in range(1, heads):
            copy_a(kind, d).wait_send()

    def sent_b(s, carry):
        @pl.when(straight(s))
        def _():
            for kind in (0, 1):
                copy_b(kind, s).wait_send()
        return carry

    lax.fori_loop(1, beyond + 1, sent_b, 0)
    if lap >= 1:
        def sent_f(s, carry):
            for kind in (0, 1):
                copy_f(kind, s).wait_send()
            return carry

        @pl.when(late)
        def _():
            lax.fori_loop(inner_n + 1, reach + 1, sent_f, 0)

    def sent_d(s, carry):
        for which in (0, 1):
            copy_d(s, which).wait_send()
        return carry

    lax.fori_loop(1, reach + 1, sent_d, 0)
    for kind in range(3):
        local_e(kind).wait()
        for d in range(1, heads):
            copy_e(kind, d).wait_send()
            arrival_e(kind, d).wait_recv()


def hand_on(a, b, c, a_to, b_to, c_to, a_via, b_via, c_via, sems):
    ways = ((a, a_via, a_to), (b, b_via, b_to), (c, c_via, c_to))
    into = [pltpu.make_async_copy(x, v, sems.at[0, i]) for i, (x, v, _) in enumerate(ways)]
    out = [pltpu.make_async_copy(v, y, sems.at[1, i]) for i, (_, v, y) in enumerate(ways)]
    for copy in into:
        copy.start()
    for before, after in zip(into, out):
        before.wait()
        after.start()
    for copy in out:
        copy.wait()


def solution(mesh):
    heads, outer_n, inner_n = (mesh.shape[a] for a in ("head", "outer", "inner"))

    def body(query_in, key_in, value_in, grad_out):
        rows = query_in.shape[1]
        tok = rows * heads
        back = min((WINDOW + tok - 2) // tok, outer_n * inner_n - 1)
        lap = back - inner_n if outer_n % 2 == 0 else -1
        lent = max(lap, 1)
        wide = GROUP * tok
        bf16, f32 = jnp.bfloat16, jnp.float32
        sem = pltpu.SemaphoreType.DMA
        shapes = [(query_in.shape[1:]), (key_in.shape[1:]), (value_in.shape[1:])]
        res = pl.pallas_call(
            functools.partial(kernel, heads, outer_n, inner_n, back, lap),
            out_shape=[jax.ShapeDtypeStruct(s, bf16) for s in shapes],
            in_specs=[pl.BlockSpec(memory_space=pl.ANY)] * 4,
            out_specs=[pl.BlockSpec(memory_space=pl.ANY)] * 3,
            scratch_shapes=[
                pltpu.VMEM((tok, GROUP * HD), bf16),
                pltpu.VMEM((tok, GROUP * HD), bf16),
                pltpu.VMEM((wide, HD), bf16),
                pltpu.VMEM((wide, HD), bf16),
                pltpu.VMEM((2, back + 1, tok, HD), bf16),
                pltpu.VMEM(((back + 1) * tok, wide), f32),
                pltpu.VMEM(((back + 1) * tok, wide), f32),
                pltpu.VMEM(((back + 1) * tok, wide), bf16),
                pltpu.VMEM((8, wide), f32),
                pltpu.VMEM((8, wide), f32),
                pltpu.VMEM((HD, wide), f32),
                pltpu.VMEM((tok, GROUP * HD), bf16),
                pltpu.VMEM((2, tok, HD), bf16),
                pltpu.VMEM((2 * tok, HD), f32),
                pltpu.VMEM((back, 2, tok, HD), bf16),
                pltpu.VMEM((back, 2, tok, HD), bf16),
                pltpu.VMEM((lent, 2, tok, HD), bf16),
                pltpu.VMEM((2, tok, HD), f32),
                sem((4, heads)), sem((4, heads)), sem((4,)),
                sem((2, back + 1)), sem((2, back + 1)), sem((2, lent + 1)),
                sem((back, 2)), sem((back, 2)), sem((lent, 2)),
                sem((3, heads)), sem((3, heads)), sem((3,)),
            ],
            compiler_params=pltpu.CompilerParams(
                collective_id=0, has_side_effects=True, vmem_limit_bytes=60 * 1024 * 1024
            ),
        )(query_in[0], key_in[0], value_in[0], grad_out[0])
        res = pl.pallas_call(
            hand_on,
            out_shape=[jax.ShapeDtypeStruct(s, bf16) for s in shapes],
            in_specs=[pl.BlockSpec(memory_space=pl.ANY)] * 3,
            out_specs=[pl.BlockSpec(memory_space=pl.ANY)] * 3,
            scratch_shapes=[pltpu.VMEM(s, bf16) for s in shapes] + [sem((2, 3))],
        )(*res)
        return tuple(r[None] for r in res)

    spec = P(("outer", "inner"), "head", None)
    return jax.shard_map(
        body, mesh=mesh, in_specs=(spec,) * 4, out_specs=(spec,) * 3, check_vma=False
    )
```

```python
import functools

import jax
import jax.numpy as jnp
from jax import lax
from jax.experimental import pallas as pl
from jax.experimental.pallas import tpu as pltpu
from jax.sharding import PartitionSpec as P

HD = 128
GROUP = 2
WINDOW = 4096
SOFT_CAP = 50.0
QUERY_SCALE = 1.0 / 12.0
LOG2E = 1.4426950408889634
MESH = pl.DeviceIdType.MESH
KT = 128
QT = 256


def dot(a, b, ca, cb):
    return lax.dot_general(a, b, (((ca,), (cb,)), ((), ())), preferred_element_type=jnp.float32)


def kernel(
    heads, outer_n, inner_n, back, lap,
    q_in, k_in, v_in, g_in,
    q_out, k_out, v_out,
    qs, gs, qst, gst, kv, e_all, w_all, d_all, tot, wgt, dqt, dq, dkv, part_sum, dsend, drecv, lent, own,
    a_send, a_recv, a_loc, b_send, b_recv, f_send, d_ssem, d_rsem, r_rsem, e_send, e_recv, e_loc,
):
    rows = q_in.shape[0]
    tok = rows * heads
    ctx = outer_n * inner_n
    h = lax.axis_index("head")
    pos = lax.axis_index("outer") * inner_n + lax.axis_index("inner")
    reach = jnp.minimum(pos, back)
    beyond = jnp.minimum(ctx - 1 - pos, back)

    def is_late(t):
        return lax.rem(lax.div(t, inner_n), 2) == 1

    late = is_late(pos)
    twin = lax.rem(jnp.where(late, pos - inner_n, pos + inner_n) + ctx, ctx)

    def at(t):
        return {"outer": lax.div(t, inner_n), "inner": lax.rem(t, inner_n)}

    def head_at(d):
        return lax.rem(h + d, heads)

    def part(who):
        return pl.ds(pl.multiple_of(who * rows, rows), rows)

    def lanes(who, width):
        return pl.ds(pl.multiple_of(who * width, width), width)

    barrier = pltpu.get_barrier_semaphore()
    for d in range(1, heads):
        pl.semaphore_signal(barrier, inc=1, device_id={"head": head_at(d)}, device_id_type=MESH)
    for s in range(1, back + 1):
        @pl.when(pos + s < ctx)
        def _():
            pl.semaphore_signal(barrier, inc=1, device_id=at(pos + s), device_id_type=MESH)

        @pl.when(pos - s >= 0)
        def _():
            pl.semaphore_signal(barrier, inc=1, device_id=at(pos - s), device_id_type=MESH)
    pl.semaphore_wait(barrier, heads - 1 + reach + beyond)

    srcs = ((k_in, HD), (v_in, HD), (q_in, GROUP * HD), (g_in, GROUP * HD))

    def dst_a(kind, who):
        if kind < 2:
            return kv.at[kind, 0, part(who)]
        return (qs if kind == 2 else gs).at[part(who)]

    def copy_a(kind, d):
        ref, width = srcs[kind]
        return pltpu.make_async_remote_copy(
            src_ref=ref.at[:, lanes(head_at(d), width)],
            dst_ref=dst_a(kind, h),
            send_sem=a_send.at[kind, d], recv_sem=a_recv.at[kind, d],
            device_id={"head": head_at(d)}, device_id_type=MESH,
        )

    def arrival_a(kind, d):
        ref, width = srcs[kind]
        return pltpu.make_async_remote_copy(
            src_ref=ref.at[:, lanes(h, width)],
            dst_ref=dst_a(kind, head_at(heads - d)),
            send_sem=a_send.at[kind, d], recv_sem=a_recv.at[kind, d],
            device_id={"head": head_at(d)}, device_id_type=MESH,
        )

    def local_a(kind):
        ref, width = srcs[kind]
        return pltpu.make_async_copy(ref.at[:, lanes(h, width)], dst_a(kind, h), a_loc.at[kind])

    def start_a(kind):
        for d in range(1, heads):
            copy_a(kind, d).start()

    def landed_a(kind):
        local_a(kind).wait()
        for d in range(1, heads):
            arrival_a(kind, d).wait_recv()

    start_a(0)

    @pl.when(late)
    def _():
        for kind in (1, 2, 3):
            start_a(kind)

    @pl.when(jnp.logical_not(late))
    def _():
        start_a(1)

    for kind in range(4):
        local_a(kind).start()

    def straight(s):
        if lap < 1:
            return pos + s < ctx
        return (pos + s < ctx) & ((s > lap) | is_late(pos + s))

    def copy_b(kind, s):
        return pltpu.make_async_remote_copy(
            src_ref=kv.at[kind, 0], dst_ref=kv.at[kind, s],
            send_sem=b_send.at[kind, s], recv_sem=b_recv.at[kind, s],
            device_id=at(lax.rem(pos + s, ctx)), device_id_type=MESH,
        )

    def copy_f(kind, s):
        return pltpu.make_async_remote_copy(
            src_ref=kv.at[kind, s], dst_ref=kv.at[kind, s - inner_n],
            send_sem=f_send.at[kind, s - inner_n], recv_sem=b_recv.at[kind, s - inner_n],
            device_id=at(twin), device_id_type=MESH,
        )

    def landed_b(kind, s):
        copy_b(kind, s).wait_recv()
        if lap >= 1:
            @pl.when(late & (s > inner_n))
            def _():
                copy_f(kind, s).start()

    tot[...] = jnp.zeros_like(tot)
    wgt[...] = jnp.zeros_like(wgt)
    dqt[...] = jnp.zeros_like(dqt)

    free = (WINDOW - tok) // tok

    def blocks(s, n):
        return pl.ds(pl.multiple_of(s * tok, tok), n * tok)

    def first(s, n, masked):
        at_s = blocks(s, n)
        keys = kv[0, pl.ds(s, n)].reshape(n * tok, HD)
        for j in range(GROUP * tok // QT):
            col = slice(j * QT, (j + 1) * QT)
            capped = jnp.tanh(dot(keys, qst[col], 1, 1) * (QUERY_SCALE / SOFT_CAP))
            e = jnp.exp2((SOFT_CAP * LOG2E) * capped)
            if masked:
                query = j * QT + lax.broadcasted_iota(jnp.int32, e.shape, 1)
                apart = (
                    s * tok + jnp.where(query >= tok, query - tok, query)
                    - lax.broadcasted_iota(jnp.int32, e.shape, 0)
                )
                e = jnp.where((apart >= 0) & (apart < WINDOW), e, 0.0)
            w_all[at_s, col] = e * (QUERY_SCALE - QUERY_SCALE * (capped * capped))
            e_all[at_s, col] = e
            tot[:, col] += jnp.sum(e.reshape(n * tok // 8, 8, QT), axis=0)

    def seen(t):
        return [slice(j * tok + t * KT, (j + 1) * tok) for j in range(GROUP)]

    def first_own():
        for t in range(tok // KT):
            at_t = slice(t * KT, (t + 1) * KT)
            keys = kv[0, 0, at_t]
            for col in seen(t):
                capped = jnp.tanh(dot(keys, qst[col], 1, 1) * (QUERY_SCALE / SOFT_CAP))
                e = jnp.exp2((SOFT_CAP * LOG2E) * capped)
                apart = (
                    lax.broadcasted_iota(jnp.int32, e.shape, 1)
                    - lax.broadcasted_iota(jnp.int32, e.shape, 0)
                )
                e = jnp.where(apart >= 0, e, 0.0)
                w_all[at_t, col] = e * (QUERY_SCALE - QUERY_SCALE * (capped * capped))
                e_all[at_t, col] = e
                tot[:, col] += jnp.sum(e.reshape(KT // 8, 8, e.shape[1]), axis=0)

    def copy_d(s, which):
        return pltpu.make_async_remote_copy(
            src_ref=dsend.at[s - 1, which], dst_ref=drecv.at[s - 1, which],
            send_sem=d_ssem.at[s - 1, which], recv_sem=d_rsem.at[s - 1, which],
            device_id=at(lax.rem(pos - s + ctx, ctx)), device_id_type=MESH,
        )

    def copy_r(s, which):
        return pltpu.make_async_remote_copy(
            src_ref=dsend.at[s - 1, which], dst_ref=lent.at[s - inner_n - 1, which],
            send_sem=d_ssem.at[s - 1, which], recv_sem=r_rsem.at[s - inner_n - 1, which],
            device_id=at(twin), device_id_type=MESH,
        )

    def arrival_r(s, which):
        return pltpu.make_async_remote_copy(
            src_ref=dsend.at[s - 1, which], dst_ref=lent.at[s - 1, which],
            send_sem=d_ssem.at[s - 1, which], recv_sem=r_rsem.at[s - 1, which],
            device_id=at(twin), device_id_type=MESH,
        )

    def give(s, n, which, value):
        part_sum[0:n * tok] = value
        for m in range(n):
            give_one(s + m, which, slice(m * tok, (m + 1) * tok))

    def give_one(s, which, rows_s):
        if lap < 1:
            dsend[s - 1, which] = part_sum[rows_s].astype(jnp.bfloat16)
            copy_d(s, which).start()
            return

        @pl.when(jnp.logical_not(late) & (s <= lap))
        def _():
            arrival_r(s, which).wait_recv()
            part_sum[rows_s] += lent[s - 1, which].astype(jnp.float32)

        dsend[s - 1, which] = part_sum[rows_s].astype(jnp.bfloat16)
        lend = late & (s > inner_n)

        @pl.when(lend)
        def _():
            copy_r(s, which).start()

        @pl.when(jnp.logical_not(lend))
        def _():
            copy_d(s, which).start()

    def first_dv(s, n):
        at_s = blocks(s, n)
        probs = [
            (e_all[at_s, j * QT:(j + 1) * QT] * tot[0:1, j * QT:(j + 1) * QT]).astype(jnp.bfloat16)
            for j in range(GROUP * tok // QT)
        ]
        give(s, n, 1, dot(jnp.concatenate(probs, axis=1), gst[...], 1, 0))

    def first_dv_own():
        for t in range(tok // KT):
            at_t = slice(t * KT, (t + 1) * KT)
            probs = [(e_all[at_t, col] * tot[0:1, col]).astype(jnp.bfloat16) for col in seen(t)]
            grads = jnp.concatenate([gst[col] for col in seen(t)], axis=0)
            own[1, at_t] = dot(jnp.concatenate(probs, axis=1), grads, 1, 0)

    def first_dp(s, n):
        for m in range(n):
            if lap >= 1:
                @pl.when(jnp.logical_not(late & (s + m > inner_n)))
                def _():
                    landed_b(1, s + m)
            else:
                landed_b(1, s + m)
        at_s = blocks(s, n)
        vals = kv[1, pl.ds(s, n)].reshape(n * tok, HD)
        for j in range(GROUP * tok // QT):
            col = slice(j * QT, (j + 1) * QT)
            dp = dot(vals, gst[col], 1, 1).astype(jnp.bfloat16)
            d_all[at_s, col] = dp
            weighted = e_all[at_s, col] * dp.astype(jnp.float32)
            wgt[:, col] += jnp.sum(weighted.reshape(n * tok // 8, 8, QT), axis=0)

    def first_dp_own():
        for t in range(tok // KT):
            at_t = slice(t * KT, (t + 1) * KT)
            vals = kv[1, 0, at_t]
            for col in seen(t):
                dp = dot(vals, gst[col], 1, 1).astype(jnp.bfloat16)
                d_all[at_t, col] = dp
                weighted = e_all[at_t, col] * dp.astype(jnp.float32)
                wgt[:, col] += jnp.sum(weighted.reshape(KT // 8, 8, weighted.shape[1]), axis=0)

    def stack(whole, stacked):
        for j in range(GROUP):
            stacked[j * tok:(j + 1) * tok] = whole[:, j * HD:(j + 1) * HD]

    def spread(kind):
        landed_a(kind)
        for s in range(1, back + 1):
            @pl.when(straight(s))
            def _():
                copy_b(kind, s).start()

    def begin():
        landed_a(2)
        stack(qs, qst)
        first_own()

    spread(0)

    pl.when(jnp.logical_not(late))(lambda: start_a(2))
    spread(1)
    pl.when(jnp.logical_not(late))(lambda: start_a(3))
    begin()

    def first_step(n, masked, base, i, carry):
        s = base + n * i
        for m in range(n):
            landed_b(0, s + m)
        first(s, n, masked)
        return carry

    edge = jnp.minimum(reach, free)
    lax.fori_loop(0, lax.div(edge, 2), functools.partial(first_step, 2, False, 1), 0)
    lax.fori_loop(edge, edge + lax.rem(edge, 2), functools.partial(first_step, 1, False, 0), 0)
    if back > free:
        lax.fori_loop(edge + 1, reach + 1, functools.partial(first_step, 1, True, 0), 0)
    inv = 1.0 / jnp.sum(tot[...], axis=0, keepdims=True)
    tot[0:1] = inv
    if lap >= 1:
        def pass_on(s, carry):
            landed_b(1, s)
            return carry

        @pl.when(late)
        def _():
            lax.fori_loop(inner_n + 1, reach + 1, pass_on, 0)
    landed_a(3)
    stack(gs, gst)

    pairs = lax.div(reach, 2)

    def in_pairs(step):
        def two(i, carry):
            step(reach - 2 * jnp.where(i == 0, 0, pairs - i) - 1, 2)
            return carry

        lax.fori_loop(0, pairs, two, 0)


    def odd_one(step):
        @pl.when(lax.rem(reach, 2) == 1)
        def _():
            step(1, 1)

    in_pairs(first_dv)
    odd_one(first_dv)
    first_dv_own()
    in_pairs(first_dp)
    odd_one(first_dp)
    first_dp_own()

    delta = jnp.sum(wgt[...], axis=0, keepdims=True) * tot[0:1]
    wgt[0:1] = delta

    def second(s, n):
        at_s = blocks(s, n)
        keys = kv[0, pl.ds(s, n)].reshape(n * tok, HD)
        scs = []
        for j in range(GROUP * tok // QT):
            col = slice(j * QT, (j + 1) * QT)
            diff = d_all[at_s, col].astype(jnp.float32) - wgt[0:1, col]
            scaled = ((w_all[at_s, col] * tot[0:1, col]) * diff).astype(jnp.bfloat16)
            dqt[:, col] += dot(keys, scaled, 0, 0)
            scs.append(scaled)
        return dot(jnp.concatenate(scs, axis=1), qst[...], 1, 0)

    def second_own():
        for t in range(tok // KT):
            at_t = slice(t * KT, (t + 1) * KT)
            scs = []
            for col in seen(t):
                diff = d_all[at_t, col].astype(jnp.float32) - wgt[0:1, col]
                scaled = ((w_all[at_t, col] * tot[0:1, col]) * diff).astype(jnp.bfloat16)
                dqt[:, col] += dot(kv[0, 0, at_t], scaled, 0, 0)
                scs.append(scaled)
            queries = jnp.concatenate([qst[col] for col in seen(t)], axis=0)
            own[0, at_t] = dot(jnp.concatenate(scs, axis=1), queries, 1, 0)

    def second_at(s, n):
        give(s, n, 0, second(s, n))

    outs = ((q_out, GROUP * HD), (k_out, HD), (v_out, HD))

    def src_e(kind, who):
        return dq.at[part(who)] if kind == 0 else dkv.at[kind - 1, part(who)]

    def copy_e(kind, d):
        ref, width = outs[kind]
        return pltpu.make_async_remote_copy(
            src_ref=src_e(kind, head_at(d)), dst_ref=ref.at[:, lanes(h, width)],
            send_sem=e_send.at[kind, d], recv_sem=e_recv.at[kind, d],
            device_id={"head": head_at(d)}, device_id_type=MESH,
        )

    def arrival_e(kind, d):
        ref, width = outs[kind]
        return pltpu.make_async_remote_copy(
            src_ref=src_e(kind, h), dst_ref=ref.at[:, lanes(head_at(heads - d), width)],
            send_sem=e_send.at[kind, d], recv_sem=e_recv.at[kind, d],
            device_id={"head": head_at(d)}, device_id_type=MESH,
        )

    def local_e(kind):
        ref, width = outs[kind]
        return pltpu.make_async_copy(src_e(kind, h), ref.at[:, lanes(h, width)], e_loc.at[kind])

    def start_e(kind):
        for d in range(1, heads):
            copy_e(kind, d).start()
        local_e(kind).start()

    def collect(which, s, carry):
        def take():
            copy_d(s, which).wait_recv()
            own[which] += drecv[s - 1, which].astype(jnp.float32)

        if lap < 1:
            take()
        else:
            pl.when(jnp.logical_not(is_late(pos + s) & (s > inner_n)))(take)
        return carry

    def hand_back(which):
        lax.fori_loop(1, beyond + 1, functools.partial(collect, which), 0)
        dkv[which] = own[which].astype(jnp.bfloat16)
        start_e(which + 1)

    last = lax.rem(pos, inner_n) == inner_n - 1
    pl.when(last)(lambda: hand_back(1))
    pl.when(late)(lambda: odd_one(second_at))
    in_pairs(second_at)
    pl.when(jnp.logical_not(late))(lambda: odd_one(second_at))
    second_own()
    for j in range(GROUP):
        dq[:, j * HD:(j + 1) * HD] = dqt[:, j * tok:(j + 1) * tok].T.astype(jnp.bfloat16)
    start_e(0)
    pl.when(jnp.logical_not(last))(lambda: hand_back(1))
    hand_back(0)

    for kind in range(4):
        for d in range(1, heads):
            copy_a(kind, d).wait_send()

    def sent_b(s, carry):
        @pl.when(straight(s))
        def _():
            for kind in (0, 1):
                copy_b(kind, s).wait_send()
        return carry

    lax.fori_loop(1, beyond + 1, sent_b, 0)
    if lap >= 1:
        def sent_f(s, carry):
            for kind in (0, 1):
                copy_f(kind, s).wait_send()
            return carry

        @pl.when(late)
        def _():
            lax.fori_loop(inner_n + 1, reach + 1, sent_f, 0)

    def sent_d(s, carry):
        for which in (0, 1):
            copy_d(s, which).wait_send()
        return carry

    lax.fori_loop(1, reach + 1, sent_d, 0)
    for kind in range(3):
        local_e(kind).wait()
        for d in range(1, heads):
            copy_e(kind, d).wait_send()
            arrival_e(kind, d).wait_recv()


def hand_on(a, b, c, a_to, b_to, c_to, a_via, b_via, c_via, sems):
    ways = ((a, a_via, a_to), (b, b_via, b_to), (c, c_via, c_to))
    into = [pltpu.make_async_copy(x, v, sems.at[0, i]) for i, (x, v, _) in enumerate(ways)]
    out = [pltpu.make_async_copy(v, y, sems.at[1, i]) for i, (_, v, y) in enumerate(ways)]
    for copy in into:
        copy.start()
    for before, after in zip(into, out):
        before.wait()
        after.start()
    for copy in out:
        copy.wait()


def solution(mesh):
    heads, outer_n, inner_n = (mesh.shape[a] for a in ("head", "outer", "inner"))

    def body(query_in, key_in, value_in, grad_out):
        rows = query_in.shape[1]
        tok = rows * heads
        back = min((WINDOW + tok - 2) // tok, outer_n * inner_n - 1)
        lap = back - inner_n if outer_n % 2 == 0 else -1
        lent = max(lap, 1)
        wide = GROUP * tok
        bf16, f32 = jnp.bfloat16, jnp.float32
        sem = pltpu.SemaphoreType.DMA
        shapes = [(query_in.shape[1:]), (key_in.shape[1:]), (value_in.shape[1:])]
        res = pl.pallas_call(
            functools.partial(kernel, heads, outer_n, inner_n, back, lap),
            out_shape=[jax.ShapeDtypeStruct(s, bf16) for s in shapes],
            in_specs=[pl.BlockSpec(memory_space=pl.ANY)] * 4,
            out_specs=[pl.BlockSpec(memory_space=pl.ANY)] * 3,
            scratch_shapes=[
                pltpu.VMEM((tok, GROUP * HD), bf16),
                pltpu.VMEM((tok, GROUP * HD), bf16),
                pltpu.VMEM((wide, HD), bf16),
                pltpu.VMEM((wide, HD), bf16),
                pltpu.VMEM((2, back + 1, tok, HD), bf16),
                pltpu.VMEM(((back + 1) * tok, wide), f32),
                pltpu.VMEM(((back + 1) * tok, wide), f32),
                pltpu.VMEM(((back + 1) * tok, wide), bf16),
                pltpu.VMEM((8, wide), f32),
                pltpu.VMEM((8, wide), f32),
                pltpu.VMEM((HD, wide), f32),
                pltpu.VMEM((tok, GROUP * HD), bf16),
                pltpu.VMEM((2, tok, HD), bf16),
                pltpu.VMEM((2 * tok, HD), f32),
                pltpu.VMEM((back, 2, tok, HD), bf16),
                pltpu.VMEM((back, 2, tok, HD), bf16),
                pltpu.VMEM((lent, 2, tok, HD), bf16),
                pltpu.VMEM((2, tok, HD), f32),
                sem((4, heads)), sem((4, heads)), sem((4,)),
                sem((2, back + 1)), sem((2, back + 1)), sem((2, lent + 1)),
                sem((back, 2)), sem((back, 2)), sem((lent, 2)),
                sem((3, heads)), sem((3, heads)), sem((3,)),
            ],
            compiler_params=pltpu.CompilerParams(
                collective_id=0, has_side_effects=True, vmem_limit_bytes=60 * 1024 * 1024
            ),
        )(query_in[0], key_in[0], value_in[0], grad_out[0])
        res = pl.pallas_call(
            hand_on,
            out_shape=[jax.ShapeDtypeStruct(s, bf16) for s in shapes],
            in_specs=[pl.BlockSpec(memory_space=pl.ANY)] * 3,
            out_specs=[pl.BlockSpec(memory_space=pl.ANY)] * 3,
            scratch_shapes=[pltpu.VMEM(s, bf16) for s in shapes] + [sem((2, 3))],
        )(*res)
        return tuple(r[None] for r in res)

    spec = P(("outer", "inner"), "head", None)
    return jax.shard_map(
        body, mesh=mesh, in_specs=(spec,) * 4, out_specs=(spec,) * 3, check_vma=False
    )
```

```python
import functools

import jax
import jax.numpy as jnp
from jax import lax
from jax.experimental import pallas as pl
from jax.experimental.pallas import tpu as pltpu
from jax.sharding import PartitionSpec as P

HD = 128
GROUP = 2
WINDOW = 4096
SOFT_CAP = 50.0
QUERY_SCALE = 1.0 / 12.0
LOG2E = 1.4426950408889634
MESH = pl.DeviceIdType.MESH
KT = 128
QT = 256


def dot(a, b, ca, cb):
    return lax.dot_general(a, b, (((ca,), (cb,)), ((), ())), preferred_element_type=jnp.float32)


def kernel(
    heads, outer_n, inner_n, back, lap,
    q_in, k_in, v_in, g_in,
    q_out, k_out, v_out,
    qs, gs, qst, gst, kv, e_all, w_all, d_all, tot, wgt, dqt, dq, dkv, part_sum, dsend, drecv, lent, own,
    a_send, a_recv, a_loc, b_send, b_recv, f_send, d_ssem, d_rsem, r_rsem, e_send, e_recv, e_loc,
):
    rows = q_in.shape[0]
    tok = rows * heads
    ctx = outer_n * inner_n
    h = lax.axis_index("head")
    pos = lax.axis_index("outer") * inner_n + lax.axis_index("inner")
    reach = jnp.minimum(pos, back)
    beyond = jnp.minimum(ctx - 1 - pos, back)

    def is_late(t):
        return lax.rem(lax.div(t, inner_n), 2) == 1

    late = is_late(pos)
    twin = lax.rem(jnp.where(late, pos - inner_n, pos + inner_n) + ctx, ctx)

    def at(t):
        return {"outer": lax.div(t, inner_n), "inner": lax.rem(t, inner_n)}

    def head_at(d):
        return lax.rem(h + d, heads)

    def part(who):
        return pl.ds(pl.multiple_of(who * rows, rows), rows)

    def lanes(who, width):
        return pl.ds(pl.multiple_of(who * width, width), width)

    barrier = pltpu.get_barrier_semaphore()
    for d in range(1, heads):
        pl.semaphore_signal(barrier, inc=1, device_id={"head": head_at(d)}, device_id_type=MESH)
    for s in range(1, back + 1):
        @pl.when(pos + s < ctx)
        def _():
            pl.semaphore_signal(barrier, inc=1, device_id=at(pos + s), device_id_type=MESH)

        @pl.when(pos - s >= 0)
        def _():
            pl.semaphore_signal(barrier, inc=1, device_id=at(pos - s), device_id_type=MESH)
    pl.semaphore_wait(barrier, heads - 1 + reach + beyond)

    srcs = ((k_in, HD), (v_in, HD), (q_in, GROUP * HD), (g_in, GROUP * HD))

    def dst_a(kind, who):
        if kind < 2:
            return kv.at[kind, 0, part(who)]
        return (qs if kind == 2 else gs).at[part(who)]

    def copy_a(kind, d):
        ref, width = srcs[kind]
        return pltpu.make_async_remote_copy(
            src_ref=ref.at[:, lanes(head_at(d), width)],
            dst_ref=dst_a(kind, h),
            send_sem=a_send.at[kind, d], recv_sem=a_recv.at[kind, d],
            device_id={"head": head_at(d)}, device_id_type=MESH,
        )

    def arrival_a(kind, d):
        ref, width = srcs[kind]
        return pltpu.make_async_remote_copy(
            src_ref=ref.at[:, lanes(h, width)],
            dst_ref=dst_a(kind, head_at(heads - d)),
            send_sem=a_send.at[kind, d], recv_sem=a_recv.at[kind, d],
            device_id={"head": head_at(d)}, device_id_type=MESH,
        )

    def local_a(kind):
        ref, width = srcs[kind]
        return pltpu.make_async_copy(ref.at[:, lanes(h, width)], dst_a(kind, h), a_loc.at[kind])

    def start_a(kind):
        for d in range(1, heads):
            copy_a(kind, d).start()

    def landed_a(kind):
        local_a(kind).wait()
        for d in range(1, heads):
            arrival_a(kind, d).wait_recv()

    start_a(0)

    @pl.when(late)
    def _():
        for kind in (1, 2, 3):
            start_a(kind)

    @pl.when(jnp.logical_not(late))
    def _():
        start_a(1)

    for kind in range(4):
        local_a(kind).start()

    def straight(s):
        if lap < 1:
            return pos + s < ctx
        return (pos + s < ctx) & ((s > lap) | is_late(pos + s))

    def copy_b(kind, s):
        return pltpu.make_async_remote_copy(
            src_ref=kv.at[kind, 0], dst_ref=kv.at[kind, s],
            send_sem=b_send.at[kind, s], recv_sem=b_recv.at[kind, s],
            device_id=at(lax.rem(pos + s, ctx)), device_id_type=MESH,
        )

    def copy_f(kind, s):
        return pltpu.make_async_remote_copy(
            src_ref=kv.at[kind, s], dst_ref=kv.at[kind, s - inner_n],
            send_sem=f_send.at[kind, s - inner_n], recv_sem=b_recv.at[kind, s - inner_n],
            device_id=at(twin), device_id_type=MESH,
        )

    def landed_b(kind, s):
        copy_b(kind, s).wait_recv()
        if lap >= 1:
            @pl.when(late & (s > inner_n))
            def _():
                copy_f(kind, s).start()

    tot[...] = jnp.zeros_like(tot)
    wgt[...] = jnp.zeros_like(wgt)
    dqt[...] = jnp.zeros_like(dqt)

    free = (WINDOW - tok) // tok

    def blocks(s, n):
        return pl.ds(pl.multiple_of(s * tok, tok), n * tok)

    def first(s, n, masked):
        at_s = blocks(s, n)
        keys = kv[0, pl.ds(s, n)].reshape(n * tok, HD)
        for j in range(GROUP * tok // QT):
            col = slice(j * QT, (j + 1) * QT)
            capped = jnp.tanh(dot(keys, qst[col], 1, 1) * (QUERY_SCALE / SOFT_CAP))
            e = jnp.exp2((SOFT_CAP * LOG2E) * capped)
            if masked:
                query = j * QT + lax.broadcasted_iota(jnp.int32, e.shape, 1)
                apart = (
                    s * tok + jnp.where(query >= tok, query - tok, query)
                    - lax.broadcasted_iota(jnp.int32, e.shape, 0)
                )
                e = jnp.where((apart >= 0) & (apart < WINDOW), e, 0.0)
            w_all[at_s, col] = e * (QUERY_SCALE - QUERY_SCALE * (capped * capped))
            e_all[at_s, col] = e
            tot[:, col] += jnp.sum(e.reshape(n * tok // 8, 8, QT), axis=0)

    def seen(t):
        return [slice(j * tok + t * KT, (j + 1) * tok) for j in range(GROUP)]

    def first_own():
        for t in range(tok // KT):
            at_t = slice(t * KT, (t + 1) * KT)
            keys = kv[0, 0, at_t]
            for col in seen(t):
                capped = jnp.tanh(dot(keys, qst[col], 1, 1) * (QUERY_SCALE / SOFT_CAP))
                e = jnp.exp2((SOFT_CAP * LOG2E) * capped)
                apart = (
                    lax.broadcasted_iota(jnp.int32, e.shape, 1)
                    - lax.broadcasted_iota(jnp.int32, e.shape, 0)
                )
                e = jnp.where(apart >= 0, e, 0.0)
                w_all[at_t, col] = e * (QUERY_SCALE - QUERY_SCALE * (capped * capped))
                e_all[at_t, col] = e
                tot[:, col] += jnp.sum(e.reshape(KT // 8, 8, e.shape[1]), axis=0)

    def copy_d(s, which):
        return pltpu.make_async_remote_copy(
            src_ref=dsend.at[s - 1, which], dst_ref=drecv.at[s - 1, which],
            send_sem=d_ssem.at[s - 1, which], recv_sem=d_rsem.at[s - 1, which],
            device_id=at(lax.rem(pos - s + ctx, ctx)), device_id_type=MESH,
        )

    def copy_r(s, which):
        return pltpu.make_async_remote_copy(
            src_ref=dsend.at[s - 1, which], dst_ref=lent.at[s - inner_n - 1, which],
            send_sem=d_ssem.at[s - 1, which], recv_sem=r_rsem.at[s - inner_n - 1, which],
            device_id=at(twin), device_id_type=MESH,
        )

    def arrival_r(s, which):
        return pltpu.make_async_remote_copy(
            src_ref=dsend.at[s - 1, which], dst_ref=lent.at[s - 1, which],
            send_sem=d_ssem.at[s - 1, which], recv_sem=r_rsem.at[s - 1, which],
            device_id=at(twin), device_id_type=MESH,
        )

    def give(s, n, which, value):
        part_sum[0:n * tok] = value
        for m in range(n):
            give_one(s + m, which, slice(m * tok, (m + 1) * tok))

    def give_one(s, which, rows_s):
        if lap < 1:
            dsend[s - 1, which] = part_sum[rows_s].astype(jnp.bfloat16)
            copy_d(s, which).start()
            return

        @pl.when(jnp.logical_not(late) & (s <= lap))
        def _():
            arrival_r(s, which).wait_recv()
            part_sum[rows_s] += lent[s - 1, which].astype(jnp.float32)

        dsend[s - 1, which] = part_sum[rows_s].astype(jnp.bfloat16)
        lend = late & (s > inner_n)

        @pl.when(lend)
        def _():
            copy_r(s, which).start()

        @pl.when(jnp.logical_not(lend))
        def _():
            copy_d(s, which).start()

    def first_dv(s, n):
        at_s = blocks(s, n)
        probs = [
            (e_all[at_s, j * QT:(j + 1) * QT] * tot[0:1, j * QT:(j + 1) * QT]).astype(jnp.bfloat16)
            for j in range(GROUP * tok // QT)
        ]
        give(s, n, 1, dot(jnp.concatenate(probs, axis=1), gst[...], 1, 0))

    def first_dv_own():
        for t in range(tok // KT):
            at_t = slice(t * KT, (t + 1) * KT)
            probs = [(e_all[at_t, col] * tot[0:1, col]).astype(jnp.bfloat16) for col in seen(t)]
            grads = jnp.concatenate([gst[col] for col in seen(t)], axis=0)
            own[1, at_t] = dot(jnp.concatenate(probs, axis=1), grads, 1, 0)

    def first_dp(s, n):
        for m in range(n):
            if lap >= 1:
                @pl.when(jnp.logical_not(late & (s + m > inner_n)))
                def _():
                    landed_b(1, s + m)
            else:
                landed_b(1, s + m)
        at_s = blocks(s, n)
        vals = kv[1, pl.ds(s, n)].reshape(n * tok, HD)
        for j in range(GROUP * tok // QT):
            col = slice(j * QT, (j + 1) * QT)
            dp = dot(vals, gst[col], 1, 1).astype(jnp.bfloat16)
            d_all[at_s, col] = dp
            weighted = e_all[at_s, col] * dp.astype(jnp.float32)
            wgt[:, col] += jnp.sum(weighted.reshape(n * tok // 8, 8, QT), axis=0)

    def first_dp_own():
        for t in range(tok // KT):
            at_t = slice(t * KT, (t + 1) * KT)
            vals = kv[1, 0, at_t]
            for col in seen(t):
                dp = dot(vals, gst[col], 1, 1).astype(jnp.bfloat16)
                d_all[at_t, col] = dp
                weighted = e_all[at_t, col] * dp.astype(jnp.float32)
                wgt[:, col] += jnp.sum(weighted.reshape(KT // 8, 8, weighted.shape[1]), axis=0)

    def stack(whole, stacked):
        for j in range(GROUP):
            stacked[j * tok:(j + 1) * tok] = whole[:, j * HD:(j + 1) * HD]

    def spread(kind):
        landed_a(kind)
        for s in range(1, back + 1):
            @pl.when(straight(s))
            def _():
                copy_b(kind, s).start()

    def begin():
        landed_a(2)
        stack(qs, qst)
        first_own()

    spread(0)

    pl.when(jnp.logical_not(late))(lambda: start_a(2))
    spread(1)
    pl.when(jnp.logical_not(late))(lambda: start_a(3))
    begin()

    def first_step(n, masked, base, i, carry):
        s = base + n * i
        for m in range(n):
            landed_b(0, s + m)
        first(s, n, masked)
        return carry

    edge = jnp.minimum(reach, free)
    lax.fori_loop(0, lax.div(edge, 2), functools.partial(first_step, 2, False, 1), 0)
    lax.fori_loop(edge, edge + lax.rem(edge, 2), functools.partial(first_step, 1, False, 0), 0)
    if back > free:
        lax.fori_loop(edge + 1, reach + 1, functools.partial(first_step, 1, True, 0), 0)
    inv = 1.0 / jnp.sum(tot[...], axis=0, keepdims=True)
    tot[0:1] = inv
    if lap >= 1:
        def pass_on(s, carry):
            landed_b(1, s)
            return carry

        @pl.when(late)
        def _():
            lax.fori_loop(inner_n + 1, reach + 1, pass_on, 0)
    landed_a(3)
    stack(gs, gst)

    pairs = lax.div(reach, 2)

    def in_pairs(step):
        def two(i, carry):
            step(reach - 2 * jnp.where(i == 0, 0, pairs - i) - 1, 2)
            return carry

        lax.fori_loop(0, pairs, two, 0)


    def odd_one(step):
        @pl.when(lax.rem(reach, 2) == 1)
        def _():
            step(1, 1)

    pl.when(late)(lambda: odd_one(first_dv))
    in_pairs(first_dv)
    pl.when(jnp.logical_not(late))(lambda: odd_one(first_dv))
    first_dv_own()
    first_dp_own()
    odd_one(first_dp)
    in_pairs(first_dp)

    delta = jnp.sum(wgt[...], axis=0, keepdims=True) * tot[0:1]
    wgt[0:1] = delta

    def second(s, n):
        at_s = blocks(s, n)
        keys = kv[0, pl.ds(s, n)].reshape(n * tok, HD)
        scs = []
        for j in range(GROUP * tok // QT):
            col = slice(j * QT, (j + 1) * QT)
            diff = d_all[at_s, col].astype(jnp.float32) - wgt[0:1, col]
            scaled = ((w_all[at_s, col] * tot[0:1, col]) * diff).astype(jnp.bfloat16)
            dqt[:, col] += dot(keys, scaled, 0, 0)
            scs.append(scaled)
        return dot(jnp.concatenate(scs, axis=1), qst[...], 1, 0)

    def second_own():
        for t in range(tok // KT):
            at_t = slice(t * KT, (t + 1) * KT)
            scs = []
            for col in seen(t):
                diff = d_all[at_t, col].astype(jnp.float32) - wgt[0:1, col]
                scaled = ((w_all[at_t, col] * tot[0:1, col]) * diff).astype(jnp.bfloat16)
                dqt[:, col] += dot(kv[0, 0, at_t], scaled, 0, 0)
                scs.append(scaled)
            queries = jnp.concatenate([qst[col] for col in seen(t)], axis=0)
            own[0, at_t] = dot(jnp.concatenate(scs, axis=1), queries, 1, 0)

    def second_at(s, n):
        give(s, n, 0, second(s, n))

    outs = ((q_out, GROUP * HD), (k_out, HD), (v_out, HD))

    def src_e(kind, who):
        return dq.at[part(who)] if kind == 0 else dkv.at[kind - 1, part(who)]

    def copy_e(kind, d):
        ref, width = outs[kind]
        return pltpu.make_async_remote_copy(
            src_ref=src_e(kind, head_at(d)), dst_ref=ref.at[:, lanes(h, width)],
            send_sem=e_send.at[kind, d], recv_sem=e_recv.at[kind, d],
            device_id={"head": head_at(d)}, device_id_type=MESH,
        )

    def arrival_e(kind, d):
        ref, width = outs[kind]
        return pltpu.make_async_remote_copy(
            src_ref=src_e(kind, h), dst_ref=ref.at[:, lanes(head_at(heads - d), width)],
            send_sem=e_send.at[kind, d], recv_sem=e_recv.at[kind, d],
            device_id={"head": head_at(d)}, device_id_type=MESH,
        )

    def local_e(kind):
        ref, width = outs[kind]
        return pltpu.make_async_copy(src_e(kind, h), ref.at[:, lanes(h, width)], e_loc.at[kind])

    def start_e(kind):
        for d in range(1, heads):
            copy_e(kind, d).start()
        local_e(kind).start()

    def collect(which, s, carry):
        def take():
            copy_d(s, which).wait_recv()
            own[which] += drecv[s - 1, which].astype(jnp.float32)

        if lap < 1:
            take()
        else:
            pl.when(jnp.logical_not(is_late(pos + s) & (s > inner_n)))(take)
        return carry

    def hand_back(which):
        lax.fori_loop(1, beyond + 1, functools.partial(collect, which), 0)
        dkv[which] = own[which].astype(jnp.bfloat16)
        start_e(which + 1)

    last = lax.rem(pos, inner_n) == inner_n - 1
    pl.when(last)(lambda: hand_back(1))
    pl.when(late)(lambda: odd_one(second_at))
    in_pairs(second_at)
    pl.when(jnp.logical_not(late))(lambda: odd_one(second_at))
    second_own()
    for j in range(GROUP):
        dq[:, j * HD:(j + 1) * HD] = dqt[:, j * tok:(j + 1) * tok].T.astype(jnp.bfloat16)
    start_e(0)
    pl.when(jnp.logical_not(last))(lambda: hand_back(1))
    hand_back(0)

    for kind in range(4):
        for d in range(1, heads):
            copy_a(kind, d).wait_send()

    def sent_b(s, carry):
        @pl.when(straight(s))
        def _():
            for kind in (0, 1):
                copy_b(kind, s).wait_send()
        return carry

    lax.fori_loop(1, beyond + 1, sent_b, 0)
    if lap >= 1:
        def sent_f(s, carry):
            for kind in (0, 1):
                copy_f(kind, s).wait_send()
            return carry

        @pl.when(late)
        def _():
            lax.fori_loop(inner_n + 1, reach + 1, sent_f, 0)

    def sent_d(s, carry):
        for which in (0, 1):
            copy_d(s, which).wait_send()
        return carry

    lax.fori_loop(1, reach + 1, sent_d, 0)
    for kind in range(3):
        local_e(kind).wait()
        for d in range(1, heads):
            copy_e(kind, d).wait_send()
            arrival_e(kind, d).wait_recv()


def hand_on(a, b, c, a_to, b_to, c_to, a_via, b_via, c_via, sems):
    ways = ((a, a_via, a_to), (b, b_via, b_to), (c, c_via, c_to))
    into = [pltpu.make_async_copy(x, v, sems.at[0, i]) for i, (x, v, _) in enumerate(ways)]
    out = [pltpu.make_async_copy(v, y, sems.at[1, i]) for i, (_, v, y) in enumerate(ways)]
    for copy in into:
        copy.start()
    for before, after in zip(into, out):
        before.wait()
        after.start()
    for copy in out:
        copy.wait()


def solution(mesh):
    heads, outer_n, inner_n = (mesh.shape[a] for a in ("head", "outer", "inner"))

    def body(query_in, key_in, value_in, grad_out):
        rows = query_in.shape[1]
        tok = rows * heads
        back = min((WINDOW + tok - 2) // tok, outer_n * inner_n - 1)
        lap = back - inner_n if outer_n % 2 == 0 else -1
        lent = max(lap, 1)
        wide = GROUP * tok
        bf16, f32 = jnp.bfloat16, jnp.float32
        sem = pltpu.SemaphoreType.DMA
        shapes = [(query_in.shape[1:]), (key_in.shape[1:]), (value_in.shape[1:])]
        res = pl.pallas_call(
            functools.partial(kernel, heads, outer_n, inner_n, back, lap),
            out_shape=[jax.ShapeDtypeStruct(s, bf16) for s in shapes],
            in_specs=[pl.BlockSpec(memory_space=pl.ANY)] * 4,
            out_specs=[pl.BlockSpec(memory_space=pl.ANY)] * 3,
            scratch_shapes=[
                pltpu.VMEM((tok, GROUP * HD), bf16),
                pltpu.VMEM((tok, GROUP * HD), bf16),
                pltpu.VMEM((wide, HD), bf16),
                pltpu.VMEM((wide, HD), bf16),
                pltpu.VMEM((2, back + 1, tok, HD), bf16),
                pltpu.VMEM(((back + 1) * tok, wide), f32),
                pltpu.VMEM(((back + 1) * tok, wide), f32),
                pltpu.VMEM(((back + 1) * tok, wide), bf16),
                pltpu.VMEM((8, wide), f32),
                pltpu.VMEM((8, wide), f32),
                pltpu.VMEM((HD, wide), f32),
                pltpu.VMEM((tok, GROUP * HD), bf16),
                pltpu.VMEM((2, tok, HD), bf16),
                pltpu.VMEM((2 * tok, HD), f32),
                pltpu.VMEM((back, 2, tok, HD), bf16),
                pltpu.VMEM((back, 2, tok, HD), bf16),
                pltpu.VMEM((lent, 2, tok, HD), bf16),
                pltpu.VMEM((2, tok, HD), f32),
                sem((4, heads)), sem((4, heads)), sem((4,)),
                sem((2, back + 1)), sem((2, back + 1)), sem((2, lent + 1)),
                sem((back, 2)), sem((back, 2)), sem((lent, 2)),
                sem((3, heads)), sem((3, heads)), sem((3,)),
            ],
            compiler_params=pltpu.CompilerParams(
                collective_id=0, has_side_effects=True, vmem_limit_bytes=60 * 1024 * 1024
            ),
        )(query_in[0], key_in[0], value_in[0], grad_out[0])
        res = pl.pallas_call(
            hand_on,
            out_shape=[jax.ShapeDtypeStruct(s, bf16) for s in shapes],
            in_specs=[pl.BlockSpec(memory_space=pl.ANY)] * 3,
            out_specs=[pl.BlockSpec(memory_space=pl.ANY)] * 3,
            scratch_shapes=[pltpu.VMEM(s, bf16) for s in shapes] + [sem((2, 3))],
        )(*res)
        return tuple(r[None] for r in res)

    spec = P(("outer", "inner"), "head", None)
    return jax.shard_map(
        body, mesh=mesh, in_specs=(spec,) * 4, out_specs=(spec,) * 3, check_vma=False
    )
```
